256 devices in a mesh: pts: 64 (over y, z, core), frq: 4 (over x).
Axes of the slice: x: 4, y: 4, z: 8, core: 2. Of those that a mesh axis runs over, the one named last changes fastest.
Arguments:
- snapshots: bfloat16 [2304, 4, 65536], P('pts', 'frq'), may hold values from -8 to 8
- weights: float32 [4, 65536], P('frq', 'pts'), may hold values from 0.1 to 3
- freq_ids: int32 [65], replicated, may hold values from 0 to 128, as said below
- starts: int32 [16], replicated, may hold values from 0 to 2047, as said below
Outputs:
- mode_field: bfloat16 [65, 2, 16, 4, 65536], P(None, None, None, 'frq', 'pts')
The draws below stay inside these ranges and needn't reach their ends.
Inputs may be any that keep to these rules, and one draw needn't show every extreme that they name: `freq_ids`: 65 distinct frequency bins of a block of 256 snapshots. Block b starts between b * 128 and b * 128 + 127; the first block starts at 0 and the last at 2047.
All inputs are finite; a program needn't handle non-finite values.
Results may differ from the reference program's by a relative error of at most 0.007.
Values may be sent and summed in bfloat16 or wider, within the bound.
A program may use at most 128 MiB of HBM per device.

```python
import math
import jax
import jax.numpy as jnp
from jax import lax

NFFT = 256
NB = 16
NF = 65
ITERS = 3
P_DEV = 1024
HOP = 128
NT = 2304
SEC = 4
P_SEC = 65536
P_ALL = 262144


def draw_snapshots(key, part):
    subkeys = jax.random.split(key, 5)
    sample_index = jnp.arange(NT, dtype=jnp.int32)[:, None, None]
    point_index = jnp.arange(SEC * P_SEC, dtype=jnp.int32).reshape(SEC, P_SEC)
    region_index = point_index // P_DEV
    region_freq = jax.random.randint(subkeys[0], (SEC * P_SEC // P_DEV,), 0, NFFT // 2 + 1)
    offset_freq = jax.random.randint(subkeys[1], (SEC, P_SEC), -2, 3)
    tone_freq = jnp.clip(region_freq[region_index] + offset_freq, 0, NFFT // 2)
    residue = tone_freq[None, :, :] * sample_index % NFFT
    phase_shift = jax.random.uniform(subkeys[2], (SEC, P_SEC), jnp.float32, -math.pi, math.pi)
    amplitude = jax.random.uniform(subkeys[3], (SEC, P_SEC), jnp.float32, 0.0, 1.5)
    noise_part = jax.random.truncated_normal(subkeys[4], -6.0, 6.0, (NT, SEC, P_SEC), jnp.float32)
    angles = 2.0 * math.pi * residue.astype(jnp.float32) / NFFT + phase_shift[None, :, :]
    return (noise_part + amplitude[None, :, :] * jnp.cos(angles)).astype(jnp.bfloat16)


def draw_weights(key, part):
    ramp_factor = 1.0 + 2.0 * jnp.arange(P_SEC, dtype=jnp.float32) / (P_SEC - 1)
    base_weight = jnp.exp(jax.random.uniform(key, (SEC, P_SEC), jnp.float32, math.log(0.1), 0.0))
    return (base_weight * ramp_factor[None, :]).astype(jnp.float32)


def draw_freq_ids(key, part):
    others = 1 + jax.random.permutation(key, NFFT // 2 - 1)[:NF - 2]
    ends = jnp.array([0, NFFT // 2], dtype=jnp.int32)
    return jnp.concatenate([ends, others.astype(jnp.int32)]).astype(jnp.int32)


def draw_starts(key, part):
    jitter = jax.random.randint(key, (NB,), 0, HOP)
    jitter = jitter.at[0].set(0).at[NB - 1].set(HOP - 1)
    return (jnp.arange(NB, dtype=jnp.int32) * HOP + jitter).astype(jnp.int32)


def setup_inputs(seed: int = 0) -> dict:
    arg_keys = jax.random.split(jax.random.key(seed), 5)
    snapshots = draw_snapshots(jax.random.fold_in(arg_keys[4], 71), 0)
    weights = draw_weights(jax.random.fold_in(arg_keys[4], 71), 0)
    freq_ids = draw_freq_ids(jax.random.fold_in(arg_keys[4], 71), 0)
    starts = draw_starts(jax.random.fold_in(arg_keys[4], 71), 0)
    return {"snapshots": snapshots, "weights": weights, "freq_ids": freq_ids, "starts": starts}


def window_table(freq_ids, length):
    sample_index = jnp.arange(length, dtype=jnp.int32)
    residue = freq_ids[:, None] * sample_index[None, :] % length
    angles = 2.0 * math.pi * residue.astype(jnp.float32) / length
    hann_window = 0.5 - 0.5 * jnp.cos(2.0 * math.pi * sample_index.astype(jnp.float32) / length)
    cos_rows = hann_window[None, :] * jnp.cos(angles)
    sin_rows = -hann_window[None, :] * jnp.sin(angles)
    return jnp.concatenate([cos_rows, sin_rows], axis=0).astype(jnp.bfloat16)

def solve_roots(real_part, imag_part, sweeps):
    order = real_part.shape[1]
    upper_half = jnp.concatenate([real_part, -imag_part], axis=2)
    lower_half = jnp.concatenate([imag_part, real_part], axis=2)
    embed = jnp.concatenate([upper_half, lower_half], axis=1)
    trace_sum = jnp.trace(real_part, axis1=1, axis2=2)
    approx = embed / trace_sum[:, None, None]
    identity = jnp.broadcast_to(jnp.eye(2 * order, dtype=jnp.float32), approx.shape)
    inverse_root = identity
    for iteration in range(sweeps):
        update = 1.5 * identity - 0.5 * jnp.matmul(inverse_root, approx, precision=lax.Precision.HIGHEST)
        approx = jnp.matmul(approx, update, precision=lax.Precision.HIGHEST)
        inverse_root = jnp.matmul(update, inverse_root, precision=lax.Precision.HIGHEST)
    root_real = inverse_root[:, :order, :order]
    root_imag = inverse_root[:, order:, :order]
    first_rows = jnp.stack([root_real, root_imag], axis=2)
    second_rows = jnp.stack([-root_imag, root_real], axis=2)
    mode_coefs = jnp.stack([first_rows, second_rows], axis=1)
    inv_scale = 1.0 / jnp.sqrt(trace_sum)
    return mode_coefs * inv_scale[:, None, None, None, None]

def gram_parts(spectra_f, weighted_f, total_points):
    gram = jnp.einsum('bkfp,clfp->fbkcl', spectra_f, weighted_f, precision=lax.Precision.HIGHEST) / total_points
    real_part = gram[:, :, 0, :, 0] + gram[:, :, 1, :, 1]
    imag_part = gram[:, :, 0, :, 1] - gram[:, :, 1, :, 0]
    return jnp.stack([real_part, imag_part], axis=0)

def reference(snapshots, weights, freq_ids, starts):
    dft_table = window_table(freq_ids, NFFT).astype(jnp.float32)
    flat_data = snapshots.reshape(NT, P_ALL)
    flat_weights = weights.reshape(P_ALL)
    block_count = P_ALL // P_DEV
    block_ids = jnp.arange(block_count, dtype=jnp.int32)

    def transform(block_index):
        columns = lax.dynamic_slice_in_dim(flat_data, block_index * P_DEV, P_DEV, 1)
        windows = jax.vmap(lambda offset: lax.dynamic_slice_in_dim(columns, offset, NFFT, 0))(starts)
        spectra = jnp.einsum('kt,btn->bkn', dft_table, windows.astype(jnp.float32), precision=lax.Precision.HIGHEST)
        spectra = spectra.astype(jnp.bfloat16).reshape(NB, 2, NF, P_DEV)
        point_weight = lax.dynamic_slice_in_dim(flat_weights, block_index * P_DEV, P_DEV, 0)
        weighted = (spectra.astype(jnp.float32) * point_weight).astype(jnp.bfloat16)
        local_gram = gram_parts(spectra.astype(jnp.float32), weighted.astype(jnp.float32), P_ALL)
        return (spectra, local_gram)
    all_spectra, all_grams = lax.map(transform, block_ids)
    gram_total = lax.optimization_barrier(jnp.sum(all_grams, axis=0))
    mode_coefs = solve_roots(gram_total[0], gram_total[1], ITERS).astype(jnp.bfloat16)
    coefs_wide = mode_coefs.astype(jnp.float32)

    def project(items):
        spectra, block_index = items
        point_weight = lax.dynamic_slice_in_dim(flat_weights, block_index * P_DEV, P_DEV, 0)
        field = jnp.einsum('bkfp,fkblm->flmp', spectra.astype(jnp.float32), coefs_wide, precision=lax.Precision.HIGHEST)
        return (field * jnp.sqrt(point_weight)).astype(jnp.bfloat16)
    fields = lax.map(project, (all_spectra, block_ids))
    fields = jnp.transpose(fields, (1, 2, 3, 0, 4))
    return fields.reshape(NF, 2, NB, SEC, P_SEC)
```

```python
import functools
import math

import jax
import jax.numpy as jnp
from jax import lax
from jax.experimental import pallas as pl
from jax.experimental.pallas import tpu as pltpu
from jax.sharding import Mesh
from jax.sharding import PartitionSpec as P

NFFT = 256
ITERS = 3
PTS = ("pts_0", "pts_1", "pts_2")
NY, NZ, NC, NX = 4, 8, 2, 4
PEERS = NY * NZ * NC
ROWS = 36
MAIN = 32
REST = ROWS - MAIN
BLOCKS = 16
FREQS = 65
GROUP = 8
GROUPS = 9
SIDE = BLOCKS * GROUP * 2
TROWS = GROUPS * GROUP * 2
POINTS = 1024
CHUNKS = 4
W = POINTS // CHUNKS
HALF = W // 2
KMAIN = 12 * MAIN
KREST = 64
TOTAL = 262144
MESH = pl.DeviceIdType.MESH
F32 = jnp.float32
BF16 = jnp.bfloat16
HIGH = lax.Precision.HIGHEST
NT = (((1,), (1,)), ((), ()))


def iota(shape, dim):
    return lax.broadcasted_iota(jnp.int32, shape, dim)


def first_source(b):
    return min(128 * b // ROWS, PEERS - 12)


def first_rest(b):
    return min(REST * first_source(b) // 16 * 16, PEERS * REST - KREST)


def same_frequency():
    return (iota((SIDE, SIDE), 0) // 2) % GROUP == (iota((SIDE, SIDE), 1) // 2) % GROUP


def spread():
    row, col = iota((SIDE, 2 * BLOCKS), 0), iota((SIDE, 2 * BLOCKS), 1)
    return (col % BLOCKS == row // (2 * GROUP)) & (col // BLOCKS == row % 2)


def first_part(shape):
    return iota(shape, len(shape) - 1) % 2 == 0


def sum_frequencies(m):
    m = m.reshape(BLOCKS, 2 * GROUP, SIDE)
    m = m[:, :8, :] + m[:, 8:, :]
    m = m + pltpu.roll(m, 4, 1)
    return m + pltpu.roll(m, 2, 1)


def first_rows(m, h3):
    m = m.reshape(BLOCKS * 8, SIDE)
    for half in range(2):
        h3[half] = m[:, 128 * half : 128 * half + 128]
    return jnp.concatenate([h3[half, pl.ds(0, BLOCKS, stride=8), :] for half in range(2)], axis=1)


def make_table(fid):
    row = iota((TROWS, FREQS), 0) // 2
    freq = jnp.sum(
        jnp.where(row == iota((TROWS, FREQS), 1), fid.astype(F32), 0.0), axis=1, keepdims=True
    ).astype(jnp.int32)
    t = iota((TROWS, NFFT), 1)
    r = iota((TROWS, NFFT), 0)
    residue = (freq * t + 64 * (r % 2)) % NFFT
    hann = 0.5 - 0.5 * jnp.cos(2.0 * math.pi * t.astype(F32) / NFFT)
    table = hann * jnp.cos(2.0 * math.pi * residue.astype(F32) / NFFT)
    return jnp.where(r // 2 < FREQS, table, 0.0).astype(BF16)


def column_times(b):
    col = iota((1, KMAIN + KREST), 1)
    main = ROWS * (first_source(b) + col // MAIN) + col % MAIN
    rest = col - KMAIN
    rest = ROWS * (first_rest(b) // REST + rest // REST) + MAIN + rest % REST
    return jnp.where(col < KMAIN, main, rest)


def solve_roots(h, group, h3):
    lane = iota((1, SIDE), 1)
    even = lane % 2 == 0
    diag = (iota((BLOCKS, SIDE), 0) == iota((BLOCKS, SIDE), 1) // (2 * GROUP)) & even
    trace = jnp.sum(jnp.where(diag, h, 0.0), axis=0, keepdims=True)
    trace = jnp.broadcast_to(trace, (8, SIDE))
    for step in (16, 32, 64, 128):
        trace = trace + pltpu.roll(trace, step, 1)
    trace = (trace + pltpu.roll(trace, 1, 1))[:1]
    trace = jnp.where(group * GROUP + (lane // 2) % GROUP < FREQS, trace, 1.0)
    rows = jnp.concatenate(
        [
            jnp.where(even, h, -h),
            jnp.where(even, pltpu.roll(h, SIDE - 1, 1), pltpu.roll(h, 1, 1)),
        ],
        axis=0,
    )
    mask = same_frequency()
    dot = functools.partial(jnp.dot, precision=HIGH, preferred_element_type=F32)
    approx = jnp.where(mask, dot(spread().astype(F32), rows / trace), 0.0)
    eye = jnp.where(iota((SIDE, SIDE), 0) == iota((SIDE, SIDE), 1), 1.5, 0.0)
    update = eye - 0.5 * approx
    root = update
    for _ in range(1, ITERS):
        approx = dot(approx, update)
        update = eye - 0.5 * dot(root, approx)
        root = dot(update, root)
    return (first_rows(sum_frequencies(root), h3) * (1.0 / jnp.sqrt(trace))).astype(BF16)


def spectra_kernel(
    x, w, fid, starts, s_out, hc,
    xs, pk, xm, xr, xu, tab, spec, gram, hsend, r1, h2, r2, hcs, h3,
    in_sem, own_main, own_rest, send_main, send_rest, recv_main, recv_rest, out_sem,
    s1_send, s1_recv, s2_send, s2_recv, s3_send, s3_recv,
):
    y, z, c = (lax.axis_index(a) for a in PTS)
    xx = lax.axis_index("frq")
    me = (y * NZ + z) * NC + c
    load = pltpu.make_async_copy(x, xs, in_sem)
    load.start()

    def at(dx, dy, dz, dc):
        return {
            "pts_0": (y + dy) % NY, "pts_1": (z + dz) % NZ, "pts_2": (c + dc) % NC,
            "frq": (xx + dx) % NX,
        }

    def plane(k):
        j, dy, dc = k % 8, (k // 8) % 4, k // 32
        dz = (1 - j % 2) * (j // 2) + (j % 2) * (8 - (j + 1) // 2)
        return at(0, dy, dz, dc)

    barrier = pltpu.get_barrier_semaphore()

    def greet(k, carry):
        pl.semaphore_signal(barrier, inc=1, device_id=plane(k), device_id_type=MESH)
        return carry

    def greet_far(k, carry):
        pl.semaphore_signal(
            barrier, inc=1, device_id=at(1 + k // 4, k % 4, 0, 0), device_id_type=MESH
        )
        return carry

    lax.fori_loop(1, PEERS, greet, 0)
    lax.fori_loop(0, 12, greet_far, 0)
    load.wait()

    low = iota((8, HALF), 0) < 4

    def pack(q, carry):
        for ch in range(CHUNKS):
            left = xs[MAIN:ROWS, pl.ds(pl.multiple_of(q * POINTS + ch * W, 128), HALF)]
            right = xs[MAIN:ROWS, pl.ds(pl.multiple_of(q * POINTS + ch * W + HALF, 128), HALF)]
            pk[q, ch] = jnp.concatenate([left.astype(F32), right.astype(F32)], axis=0).astype(BF16)
        return carry

    lax.fori_loop(0, PEERS, pack, 0)
    pl.semaphore_wait(barrier, PEERS - 1 + 12)

    for ch in range(CHUNKS):
        pltpu.make_async_copy(
            xs.at[0:MAIN, pl.ds(pl.multiple_of(me * POINTS + ch * W, 128), W)],
            xm.at[ch, pl.ds(pl.multiple_of(me * MAIN, MAIN), MAIN), :],
            own_main.at[ch],
        ).start()
        pltpu.make_async_copy(pk.at[me, ch], xr.at[ch, me], own_rest.at[ch]).start()

        def send(k, carry):
            to = plane(k)
            q = (to["pts_0"] * NZ + to["pts_1"]) * NC + to["pts_2"]
            pltpu.make_async_remote_copy(
                src_ref=xs.at[0:MAIN, pl.ds(pl.multiple_of(q * POINTS + ch * W, 128), W)],
                dst_ref=xm.at[ch, pl.ds(pl.multiple_of(me * MAIN, MAIN), MAIN), :],
                send_sem=send_main.at[ch], recv_sem=recv_main.at[ch],
                device_id=to, device_id_type=MESH,
            ).start()
            pltpu.make_async_remote_copy(
                src_ref=pk.at[q, ch], dst_ref=xr.at[ch, me],
                send_sem=send_rest.at[ch], recv_sem=recv_rest.at[ch],
                device_id=to, device_id_type=MESH,
            ).start()
            return carry

        lax.fori_loop(1, PEERS, send, 0)

    table = make_table(fid[...])
    tau = iota((NFFT, KMAIN + KREST), 0)
    for b in range(BLOCKS):
        pick = jnp.where(tau == column_times(b) - starts[b], 1.0, 0.0).astype(BF16)
        tab[b] = jnp.dot(table, pick, preferred_element_type=F32).astype(BF16)

    def finished(ref, sem):
        pltpu.make_async_copy(ref, ref, sem).wait()

    gram[...] = jnp.zeros_like(gram)

    def chunk(ch, carry):
        finished(xm.at[ch, pl.ds(0, MAIN), :], own_main.at[ch])
        finished(xr.at[ch, 0], own_rest.at[ch])
        finished(xm.at[ch, pl.ds(0, (PEERS - 1) * MAIN), :], recv_main.at[ch])
        finished(xr.at[ch, pl.ds(0, PEERS - 1)], recv_rest.at[ch])
        rest = xr[ch].astype(F32).reshape(PEERS // 2, 2, 8, HALF)
        first, second = rest[:, 0], rest[:, 1]
        top = iota((PEERS // 2, 8, HALF), 1) < 4
        left = jnp.where(top, first, pltpu.roll(second, 4, 1))
        right = jnp.where(top, pltpu.roll(first, 4, 1), second)
        xu[:, :HALF] = left.reshape(PEERS * REST, HALF).astype(BF16)
        xu[:, HALF:] = right.reshape(PEERS * REST, HALF).astype(BF16)
        for b in range(BLOCKS):
            s0, r0 = MAIN * first_source(b), first_rest(b)
            part = jnp.concatenate([xm[ch, s0 : s0 + KMAIN, :], xu[r0 : r0 + KREST, :]], axis=0)
            rows = jnp.dot(tab[b], part, preferred_element_type=F32).astype(BF16)
            for g in range(GROUPS):
                spec[ch, g, 16 * b : 16 * b + 16, :] = rows[16 * g : 16 * g + 16, :]
        weight = w[:, pl.ds(pl.multiple_of(ch * W, W), W)]
        for g in range(GROUPS):
            s = spec[ch, g]
            weighted = (s.astype(F32) * weight).astype(BF16)
            gram[g] += lax.dot_general(s, weighted, NT, preferred_element_type=F32)
        pltpu.make_async_copy(
            spec.at[ch], s_out.at[:, :, pl.ds(pl.multiple_of(ch * W, W), W)], out_sem.at[ch]
        ).start()
        return carry

    lax.fori_loop(0, CHUNKS, chunk, 0)

    mask = same_frequency()
    even3 = first_part((BLOCKS, 8, SIDE))
    for g in range(GROUPS):
        m = sum_frequencies(jnp.where(mask, gram[g], 0.0))
        other = pltpu.roll(m, 7, 1)
        m = jnp.where(even3, m + pltpu.roll(other, SIDE - 1, 2), m - pltpu.roll(other, 1, 2))
        hsend[g] = first_rows(m, h3.at[g % 2]) * (1.0 / TOTAL)

    mine = jnp.where(c == 0, z, GROUPS - 1)
    owner = (c == 0) | (z == 0)
    here = z * NC + c

    def stage1(g):
        oz, oc = (g, 0) if g < NZ else (0, 1)
        return pltpu.make_async_remote_copy(
            src_ref=hsend.at[g], dst_ref=r1.at[here], send_sem=s1_send.at[g], recv_sem=s1_recv,
            device_id={"pts_0": y, "pts_1": oz, "pts_2": oc, "frq": xx}, device_id_type=MESH,
        )

    def elsewhere(g):
        return (z != g) | (c != 0) if g < NZ else (z != 0) | (c != 1)

    for g in range(GROUPS):
        @pl.when(elsewhere(g))
        def _():
            stage1(g).start()

    def stage2(k):
        return pltpu.make_async_remote_copy(
            src_ref=h2, dst_ref=r2.at[xx * NY + y], send_sem=s2_send, recv_sem=s2_recv,
            device_id=at(k // 4, k % 4, 0, 0), device_id_type=MESH,
        )

    def stage3(k):
        return pltpu.make_async_remote_copy(
            src_ref=hcs, dst_ref=hc.at[mine], send_sem=s3_send, recv_sem=s3_recv.at[mine],
            device_id=at(0, 0, k // 2, k % 2), device_id_type=MESH,
        )

    @pl.when(owner)
    def _():
        r1[here] = hsend[mine]
        finished(r1.at[pl.ds(0, 15)], s1_recv)
        total = r1[0]
        for i in range(1, 16):
            total = total + r1[i]
        h2[...] = total
        r2[xx * NY + y] = total

        def out2(k, carry):
            stage2(k).start()
            return carry

        lax.fori_loop(1, 16, out2, 0)
        finished(r2.at[pl.ds(0, 15)], s2_recv)
        total = r2[0]
        for i in range(1, 16):
            total = total + r2[i]
        coefs = solve_roots(total, mine, h3.at[0])
        hcs[...] = coefs
        hc[mine] = coefs

        def out3(k, carry):
            stage3(k).start()
            return carry

        lax.fori_loop(1, 16, out3, 0)
        finished(r2.at[pl.ds(0, 15)], s2_send)

    for g in range(GROUPS):
        @pl.when(elsewhere(g))
        def _():
            stage1(g).wait_send()
            finished(hc.at[g], s3_recv.at[g])

    @pl.when(owner)
    def _():
        finished(xm.at[0, pl.ds(0, 15 * BLOCKS), :], s3_send)

    for ch in range(CHUNKS):
        finished(xm.at[ch, pl.ds(0, (PEERS - 1) * MAIN), :], send_main.at[ch])
        finished(xr.at[ch, pl.ds(0, PEERS - 1)], send_rest.at[ch])
        pltpu.make_async_copy(
            spec.at[ch], s_out.at[:, :, pl.ds(ch * W, W)], out_sem.at[ch]
        ).wait()


def project_kernel(hc, s, w, out):
    h = hc[0].astype(F32)
    even = first_part((1, SIDE))
    rows = jnp.concatenate(
        [
            jnp.where(even, h, -h),
            jnp.where(even, pltpu.roll(h, SIDE - 1, 1), pltpu.roll(h, 1, 1)),
        ],
        axis=0,
    ).astype(BF16)
    coefs = jnp.dot(spread().astype(F32).astype(BF16), rows, preferred_element_type=F32)
    coefs = jnp.where(same_frequency(), coefs, 0.0).astype(BF16)
    row, col = iota((SIDE, SIDE), 0), iota((SIDE, SIDE), 1)
    order = jnp.where(
        col == (row % 16) * 16 + (row // 32) * 2 + (row // 16) % 2, 1.0, 0.0
    ).astype(BF16)
    matrix = lax.dot_general(order, coefs, NT, preferred_element_type=F32).astype(BF16)
    field = jnp.dot(matrix, s[0], preferred_element_type=F32)
    out[...] = (field * jnp.sqrt(w[...])).astype(BF16)


def shards(snapshots, weights, freq_ids, starts):
    vmem = pl.BlockSpec(memory_space=pltpu.VMEM)
    anywhere = pl.BlockSpec(memory_space=pl.ANY)
    dma = pltpu.SemaphoreType.DMA
    spectra, coefs = pl.pallas_call(
        spectra_kernel,
        name="exchange_spectra",
        out_shape=(
            jax.ShapeDtypeStruct((GROUPS, SIDE, POINTS), BF16),
            jax.ShapeDtypeStruct((GROUPS, BLOCKS, SIDE), BF16),
        ),
        in_specs=[anywhere, vmem, vmem, pl.BlockSpec(memory_space=pltpu.SMEM)],
        out_specs=(anywhere, vmem),
        scratch_shapes=[
            pltpu.VMEM((ROWS, PEERS * POINTS), BF16),
            pltpu.VMEM((PEERS, CHUNKS, 8, HALF), BF16),
            pltpu.VMEM((CHUNKS, PEERS * MAIN, W), BF16),
            pltpu.VMEM((CHUNKS, PEERS, 8, HALF), BF16),
            pltpu.VMEM((PEERS * REST, W), BF16),
            pltpu.VMEM((BLOCKS, TROWS, KMAIN + KREST), BF16),
            pltpu.VMEM((CHUNKS, GROUPS, SIDE, W), BF16),
            pltpu.VMEM((GROUPS, SIDE, SIDE), F32),
            pltpu.VMEM((GROUPS, BLOCKS, SIDE), F32),
            pltpu.VMEM((16, BLOCKS, SIDE), F32),
            pltpu.VMEM((BLOCKS, SIDE), F32),
            pltpu.VMEM((16, BLOCKS, SIDE), F32),
            pltpu.VMEM((BLOCKS, SIDE), BF16),
            pltpu.VMEM((2, 2, BLOCKS * 8, 128), F32),
            dma(()), dma((CHUNKS,)), dma((CHUNKS,)), dma((CHUNKS,)), dma((CHUNKS,)),
            dma((CHUNKS,)), dma((CHUNKS,)), dma((CHUNKS,)),
            dma((GROUPS,)), dma(()), dma(()), dma(()), dma(()), dma((GROUPS,)),
        ],
        compiler_params=pltpu.CompilerParams(
            collective_id=0, has_side_effects=True, vmem_limit_bytes=56 << 20
        ),
    )(snapshots.reshape(ROWS, PEERS * POINTS), weights, freq_ids.reshape(1, FREQS), starts)
    field = pl.pallas_call(
        project_kernel,
        name="project_modes",
        grid=(GROUPS,),
        out_shape=jax.ShapeDtypeStruct((FREQS * 2 * BLOCKS, POINTS), BF16),
        in_specs=[
            pl.BlockSpec((1, BLOCKS, SIDE), lambda g: (g, 0, 0)),
            pl.BlockSpec((1, SIDE, POINTS), lambda g: (g, 0, 0)),
            pl.BlockSpec((1, POINTS), lambda g: (0, 0)),
        ],
        out_specs=pl.BlockSpec((SIDE, POINTS), lambda g: (g, 0)),
    )(coefs, spectra, weights)
    return field.reshape(FREQS, 2, BLOCKS, 1, POINTS)


def solution(mesh):
    torus = Mesh(
        mesh.devices.reshape(NY, NZ, NC, mesh.shape["frq"]), ("pts_0", "pts_1", "pts_2", "frq")
    )
    placed = (P(PTS, "frq", None), P("frq", PTS), P(), P())
    return jax.shard_map(
        shards,
        mesh=torus,
        in_specs=placed,
        out_specs=P(None, None, None, "frq", PTS),
        check_vma=False,
    )
```

```python
import functools
import math

import jax
import jax.numpy as jnp
from jax import lax
from jax.experimental import pallas as pl
from jax.experimental.pallas import tpu as pltpu
from jax.sharding import Mesh
from jax.sharding import PartitionSpec as P

NFFT = 256
ITERS = 3
PTS = ("pts_0", "pts_1", "pts_2")
NY, NZ, NC, NX = 4, 8, 2, 4
PEERS = NY * NZ * NC
ROWS = 36
MAIN = 32
REST = ROWS - MAIN
BLOCKS = 16
FREQS = 65
GROUP = 8
GROUPS = 9
SIDE = BLOCKS * GROUP * 2
TROWS = GROUPS * GROUP * 2
POINTS = 1024
CHUNKS = 4
W = POINTS // CHUNKS
HALF = W // 2
KMAIN = 12 * MAIN
KREST = 64
TOTAL = 262144
MESH = pl.DeviceIdType.MESH
F32 = jnp.float32
BF16 = jnp.bfloat16
HIGH = lax.Precision.HIGHEST
NT = (((1,), (1,)), ((), ()))


def iota(shape, dim):
    return lax.broadcasted_iota(jnp.int32, shape, dim)


def first_source(b):
    return min(128 * b // ROWS, PEERS - 12)


def first_rest(b):
    return min(REST * first_source(b) // 16 * 16, PEERS * REST - KREST)


def same_frequency():
    return (iota((SIDE, SIDE), 0) // 2) % GROUP == (iota((SIDE, SIDE), 1) // 2) % GROUP


def spread():
    row, col = iota((SIDE, 2 * BLOCKS), 0), iota((SIDE, 2 * BLOCKS), 1)
    return (col % BLOCKS == row // (2 * GROUP)) & (col // BLOCKS == row % 2)


def first_part(shape):
    return iota(shape, len(shape) - 1) % 2 == 0


def sum_frequencies(m):
    m = m.reshape(BLOCKS, 2 * GROUP, SIDE)
    m = m[:, :8, :] + m[:, 8:, :]
    m = m + pltpu.roll(m, 4, 1)
    return m + pltpu.roll(m, 2, 1)


def first_rows(m, h3):
    m = m.reshape(BLOCKS * 8, SIDE)
    for half in range(2):
        h3[half] = m[:, 128 * half : 128 * half + 128]
    return jnp.concatenate([h3[half, pl.ds(0, BLOCKS, stride=8), :] for half in range(2)], axis=1)


def make_table(fid):
    row = iota((TROWS, FREQS), 0) // 2
    freq = jnp.sum(
        jnp.where(row == iota((TROWS, FREQS), 1), fid.astype(F32), 0.0), axis=1, keepdims=True
    ).astype(jnp.int32)
    t = iota((TROWS, NFFT), 1)
    r = iota((TROWS, NFFT), 0)
    residue = (freq * t + 64 * (r % 2)) % NFFT
    hann = 0.5 - 0.5 * jnp.cos(2.0 * math.pi * t.astype(F32) / NFFT)
    table = hann * jnp.cos(2.0 * math.pi * residue.astype(F32) / NFFT)
    return jnp.where(r // 2 < FREQS, table, 0.0).astype(BF16)


def column_times(b):
    col = iota((1, KMAIN + KREST), 1)
    main = ROWS * (first_source(b) + col // MAIN) + col % MAIN
    rest = col - KMAIN
    rest = ROWS * (first_rest(b) // REST + rest // REST) + MAIN + rest % REST
    return jnp.where(col < KMAIN, main, rest)


def solve_roots(h, group, h3):
    lane = iota((1, SIDE), 1)
    even = lane % 2 == 0
    diag = (iota((BLOCKS, SIDE), 0) == iota((BLOCKS, SIDE), 1) // (2 * GROUP)) & even
    trace = jnp.sum(jnp.where(diag, h, 0.0), axis=0, keepdims=True)
    trace = jnp.broadcast_to(trace, (8, SIDE))
    for step in (16, 32, 64, 128):
        trace = trace + pltpu.roll(trace, step, 1)
    trace = (trace + pltpu.roll(trace, 1, 1))[:1]
    trace = jnp.where(group * GROUP + (lane // 2) % GROUP < FREQS, trace, 1.0)
    rows = jnp.concatenate(
        [
            jnp.where(even, h, -h),
            jnp.where(even, pltpu.roll(h, SIDE - 1, 1), pltpu.roll(h, 1, 1)),
        ],
        axis=0,
    )
    mask = same_frequency()
    dot = functools.partial(jnp.dot, precision=HIGH, preferred_element_type=F32)
    approx = jnp.where(mask, dot(spread().astype(F32), rows / trace), 0.0)
    eye = jnp.where(iota((SIDE, SIDE), 0) == iota((SIDE, SIDE), 1), 1.5, 0.0)
    update = eye - 0.5 * approx
    root = update
    for _ in range(1, ITERS):
        approx = dot(approx, update)
        update = eye - 0.5 * dot(root, approx)
        root = dot(update, root)
    return (first_rows(sum_frequencies(root), h3) * (1.0 / jnp.sqrt(trace))).astype(BF16)


def spectra_kernel(
    x, w, fid, starts, spec, hc,
    xs, pk, xm, xr, xu, tab, gram, hsend, r1, h2, r2, hcs, h3,
    in_sem, own_main, own_rest, send_main, send_rest, recv_main, recv_rest,
    s1_send, s1_recv, s2_send, s2_recv, s3_send, s3_recv,
):
    y, z, c = (lax.axis_index(a) for a in PTS)
    xx = lax.axis_index("frq")
    me = (y * NZ + z) * NC + c
    load = pltpu.make_async_copy(x, xs, in_sem)
    load.start()

    def at(dx, dy, dz, dc):
        return {
            "pts_0": (y + dy) % NY, "pts_1": (z + dz) % NZ, "pts_2": (c + dc) % NC,
            "frq": (xx + dx) % NX,
        }

    def plane(k):
        j, dy, dc = k % 8, (k // 8) % 4, k // 32
        dz = (1 - j % 2) * (j // 2) + (j % 2) * (8 - (j + 1) // 2)
        return at(0, dy, dz, dc)

    barrier = pltpu.get_barrier_semaphore()

    def greet(k, carry):
        pl.semaphore_signal(barrier, inc=1, device_id=plane(k), device_id_type=MESH)
        return carry

    def greet_far(k, carry):
        pl.semaphore_signal(
            barrier, inc=1, device_id=at(1 + k // 4, k % 4, 0, 0), device_id_type=MESH
        )
        return carry

    for k in range(12):
        greet_far(k, 0)
    for k in range(PEERS - 1, 0, -1):
        greet(k, 0)
    load.wait()

    low = iota((8, HALF), 0) < 4

    def pack(q, carry):
        for ch in range(CHUNKS):
            left = xs[MAIN:ROWS, pl.ds(pl.multiple_of(q * POINTS + ch * W, 128), HALF)]
            right = xs[MAIN:ROWS, pl.ds(pl.multiple_of(q * POINTS + ch * W + HALF, 128), HALF)]
            pk[q, ch] = jnp.concatenate([left.astype(F32), right.astype(F32)], axis=0).astype(BF16)
        return carry

    lax.fori_loop(0, PEERS, pack, 0)
    pl.semaphore_wait(barrier, PEERS - 1 + 12)

    for ch in range(CHUNKS):
        pltpu.make_async_copy(
            xs.at[0:MAIN, pl.ds(pl.multiple_of(me * POINTS + ch * W, 128), W)],
            xm.at[ch, pl.ds(pl.multiple_of(me * MAIN, MAIN), MAIN), :],
            own_main.at[ch],
        ).start()
        pltpu.make_async_copy(pk.at[me, ch], xr.at[ch, me], own_rest.at[ch]).start()

        def send(k, carry):
            to = plane(k)
            q = (to["pts_0"] * NZ + to["pts_1"]) * NC + to["pts_2"]
            pltpu.make_async_remote_copy(
                src_ref=xs.at[0:MAIN, pl.ds(pl.multiple_of(q * POINTS + ch * W, 128), W)],
                dst_ref=xm.at[ch, pl.ds(pl.multiple_of(me * MAIN, MAIN), MAIN), :],
                send_sem=send_main.at[ch], recv_sem=recv_main.at[ch],
                device_id=to, device_id_type=MESH,
            ).start()
            pltpu.make_async_remote_copy(
                src_ref=pk.at[q, ch], dst_ref=xr.at[ch, me],
                send_sem=send_rest.at[ch], recv_sem=recv_rest.at[ch],
                device_id=to, device_id_type=MESH,
            ).start()
            return carry

        lax.fori_loop(1, PEERS, send, 0)

    table = make_table(fid[...])
    tau = iota((NFFT, KMAIN + KREST), 0)
    for b in range(BLOCKS):
        pick = jnp.where(tau == column_times(b) - starts[b], 1.0, 0.0).astype(BF16)
        tab[b] = jnp.dot(table, pick, preferred_element_type=F32).astype(BF16)

    def finished(ref, sem):
        pltpu.make_async_copy(ref, ref, sem).wait()

    gram[...] = jnp.zeros_like(gram)

    def chunk(ch, carry):
        here = pl.ds(pl.multiple_of(ch * W, W), W)
        finished(xm.at[ch, pl.ds(0, MAIN), :], own_main.at[ch])
        finished(xr.at[ch, 0], own_rest.at[ch])
        finished(xm.at[ch, pl.ds(0, (PEERS - 1) * MAIN), :], recv_main.at[ch])
        finished(xr.at[ch, pl.ds(0, PEERS - 1)], recv_rest.at[ch])
        rest = xr[ch].astype(F32).reshape(PEERS // 2, 2, 8, HALF)
        first, second = rest[:, 0], rest[:, 1]
        top = iota((PEERS // 2, 8, HALF), 1) < 4
        left = jnp.where(top, first, pltpu.roll(second, 4, 1))
        right = jnp.where(top, pltpu.roll(first, 4, 1), second)
        xu[:, :HALF] = left.reshape(PEERS * REST, HALF).astype(BF16)
        xu[:, HALF:] = right.reshape(PEERS * REST, HALF).astype(BF16)
        for b in range(BLOCKS):
            s0, r0 = MAIN * first_source(b), first_rest(b)
            part = jnp.concatenate([xm[ch, s0 : s0 + KMAIN, :], xu[r0 : r0 + KREST, :]], axis=0)
            rows = jnp.dot(tab[b], part, preferred_element_type=F32).astype(BF16)
            for g in range(GROUPS):
                spec[g, 16 * b : 16 * b + 16, here] = rows[16 * g : 16 * g + 16, :]
        weight = w[:, here]
        for g in range(GROUPS):
            s = spec[g, :, here]
            weighted = (s.astype(F32) * weight).astype(BF16)
            gram[g] += lax.dot_general(s, weighted, NT, preferred_element_type=F32)
        return carry

    lax.fori_loop(0, CHUNKS, chunk, 0)

    mask = same_frequency()
    even3 = first_part((BLOCKS, 8, SIDE))
    for g in range(GROUPS):
        m = sum_frequencies(jnp.where(mask, gram[g], 0.0))
        other = pltpu.roll(m, 7, 1)
        m = jnp.where(even3, m + pltpu.roll(other, SIDE - 1, 2), m - pltpu.roll(other, 1, 2))
        hsend[g] = first_rows(m, h3.at[g % 2]) * (1.0 / TOTAL)

    mine = jnp.where(c == 0, z, GROUPS - 1)
    owner = (c == 0) | (z == 0)
    here = z * NC + c

    def stage1(g):
        oz, oc = (g, 0) if g < NZ else (0, 1)
        return pltpu.make_async_remote_copy(
            src_ref=hsend.at[g], dst_ref=r1.at[here], send_sem=s1_send.at[g], recv_sem=s1_recv,
            device_id={"pts_0": y, "pts_1": oz, "pts_2": oc, "frq": xx}, device_id_type=MESH,
        )

    def elsewhere(g):
        return (z != g) | (c != 0) if g < NZ else (z != 0) | (c != 1)

    for g in range(GROUPS):
        @pl.when(elsewhere(g))
        def _():
            stage1(g).start()

    def stage2(k):
        return pltpu.make_async_remote_copy(
            src_ref=h2, dst_ref=r2.at[xx * NY + y], send_sem=s2_send, recv_sem=s2_recv,
            device_id=at(k // 4, k % 4, 0, 0), device_id_type=MESH,
        )

    def stage3(k):
        return pltpu.make_async_remote_copy(
            src_ref=hcs, dst_ref=hc.at[mine], send_sem=s3_send, recv_sem=s3_recv.at[mine],
            device_id=at(0, 0, k // 2, k % 2), device_id_type=MESH,
        )

    @pl.when(owner)
    def _():
        r1[here] = hsend[mine]
        finished(r1.at[pl.ds(0, 15)], s1_recv)
        total = r1[0]
        for i in range(1, 16):
            total = total + r1[i]
        h2[...] = total
        r2[xx * NY + y] = total

        def out2(k, carry):
            stage2(k).start()
            return carry

        lax.fori_loop(1, 16, out2, 0)
        finished(r2.at[pl.ds(0, 15)], s2_recv)
        total = r2[0]
        for i in range(1, 16):
            total = total + r2[i]
        coefs = solve_roots(total, mine, h3.at[0])
        hcs[...] = coefs
        hc[mine] = coefs

        def out3(k, carry):
            stage3(k).start()
            return carry

        lax.fori_loop(1, 16, out3, 0)
        finished(r2.at[pl.ds(0, 15)], s2_send)

    for g in range(GROUPS):
        @pl.when(elsewhere(g))
        def _():
            stage1(g).wait_send()
            finished(hc.at[g], s3_recv.at[g])

    @pl.when(owner)
    def _():
        finished(xm.at[0, pl.ds(0, 15 * BLOCKS), :], s3_send)

    for ch in range(CHUNKS):
        finished(xm.at[ch, pl.ds(0, (PEERS - 1) * MAIN), :], send_main.at[ch])
        finished(xr.at[ch, pl.ds(0, PEERS - 1)], send_rest.at[ch])


def project_kernel(hc, s, w, out, fields, sem):
    even = first_part((1, SIDE))
    expand = spread().astype(F32).astype(BF16)
    mask = same_frequency()
    row, col = iota((SIDE, SIDE), 0), iota((SIDE, SIDE), 1)
    order = jnp.where(
        col == (row % 16) * 16 + (row // 32) * 2 + (row // 16) % 2, 1.0, 0.0
    ).astype(BF16)
    root = jnp.sqrt(w[...])
    copies = []
    for g in range(GROUPS):
        h = hc[g].astype(F32)
        rows = jnp.concatenate(
            [
                jnp.where(even, h, -h),
                jnp.where(even, pltpu.roll(h, SIDE - 1, 1), pltpu.roll(h, 1, 1)),
            ],
            axis=0,
        ).astype(BF16)
        coefs = jnp.dot(expand, rows, preferred_element_type=F32)
        coefs = jnp.where(mask, coefs, 0.0).astype(BF16)
        count = min(SIDE, (FREQS - g * GROUP) * 2 * BLOCKS)
        matrix = lax.dot_general(order[:count], coefs, NT, preferred_element_type=F32)
        field = jnp.dot(matrix.astype(BF16), s[g], preferred_element_type=F32)
        fields[g, :count] = (field * root).astype(BF16)
        copies.append(
            pltpu.make_async_copy(
                fields.at[g, pl.ds(0, count)], out.at[pl.ds(g * SIDE, count)], sem.at[g]
            )
        )
        copies[-1].start()
    for copy in copies:
        copy.wait()


def shards(snapshots, weights, freq_ids, starts):
    vmem = pl.BlockSpec(memory_space=pltpu.VMEM)
    anywhere = pl.BlockSpec(memory_space=pl.ANY)
    dma = pltpu.SemaphoreType.DMA
    spectra, coefs = pl.pallas_call(
        spectra_kernel,
        name="exchange_spectra",
        out_shape=(
            pltpu.VMEM((GROUPS, SIDE, POINTS), BF16),
            pltpu.VMEM((GROUPS, BLOCKS, SIDE), BF16),
        ),
        in_specs=[anywhere, vmem, vmem, pl.BlockSpec(memory_space=pltpu.SMEM)],
        out_specs=(vmem, vmem),
        scratch_shapes=[
            pltpu.VMEM((ROWS, PEERS * POINTS), BF16),
            pltpu.VMEM((PEERS, CHUNKS, 8, HALF), BF16),
            pltpu.VMEM((CHUNKS, PEERS * MAIN, W), BF16),
            pltpu.VMEM((CHUNKS, PEERS, 8, HALF), BF16),
            pltpu.VMEM((PEERS * REST, W), BF16),
            pltpu.VMEM((BLOCKS, TROWS, KMAIN + KREST), BF16),
            pltpu.VMEM((GROUPS, SIDE, SIDE), F32),
            pltpu.VMEM((GROUPS, BLOCKS, SIDE), F32),
            pltpu.VMEM((16, BLOCKS, SIDE), F32),
            pltpu.VMEM((BLOCKS, SIDE), F32),
            pltpu.VMEM((16, BLOCKS, SIDE), F32),
            pltpu.VMEM((BLOCKS, SIDE), BF16),
            pltpu.VMEM((2, 2, BLOCKS * 8, 128), F32),
            dma(()), dma((CHUNKS,)), dma((CHUNKS,)), dma((CHUNKS,)), dma((CHUNKS,)),
            dma((CHUNKS,)), dma((CHUNKS,)),
            dma((GROUPS,)), dma(()), dma(()), dma(()), dma(()), dma((GROUPS,)),
        ],
        compiler_params=pltpu.CompilerParams(
            collective_id=0, has_side_effects=True, vmem_limit_bytes=56 << 20
        ),
    )(snapshots.reshape(ROWS, PEERS * POINTS), weights, freq_ids.reshape(1, FREQS), starts)
    field = pl.pallas_call(
        project_kernel,
        name="project_modes",
        out_shape=jax.ShapeDtypeStruct((FREQS * 2 * BLOCKS, POINTS), BF16),
        in_specs=[vmem, vmem, vmem],
        out_specs=anywhere,
        scratch_shapes=[pltpu.VMEM((GROUPS, SIDE, POINTS), BF16), dma((GROUPS,))],
        compiler_params=pltpu.CompilerParams(vmem_limit_bytes=24 << 20),
    )(coefs, spectra, weights)
    return field.reshape(FREQS, 2, BLOCKS, 1, POINTS)


def solution(mesh):
    torus = Mesh(
        mesh.devices.reshape(NY, NZ, NC, mesh.shape["frq"]), ("pts_0", "pts_1", "pts_2", "frq")
    )
    placed = (P(PTS, "frq", None), P("frq", PTS), P(), P())
    return jax.shard_map(
        shards,
        mesh=torus,
        in_specs=placed,
        out_specs=P(None, None, None, "frq", PTS),
        check_vma=False,
    )
```

```python
import functools
import math

import jax
import jax.numpy as jnp
from jax import lax
from jax.experimental import pallas as pl
from jax.experimental.pallas import tpu as pltpu
from jax.sharding import Mesh
from jax.sharding import PartitionSpec as P

NFFT = 256
ITERS = 3
PTS = ("pts_0", "pts_1", "pts_2")
NY, NZ, NC, NX = 4, 8, 2, 4
PEERS = NY * NZ * NC
ROWS = 36
MAIN = 32
REST = ROWS - MAIN
BLOCKS = 16
FREQS = 65
GROUP = 8
GROUPS = 9
SIDE = BLOCKS * GROUP * 2
TROWS = GROUPS * GROUP * 2
POINTS = 1024
CHUNKS = 4
W = POINTS // CHUNKS
HALF = W // 2
KMAIN = 12 * MAIN
KREST = 64
TOTAL = 262144
MESH = pl.DeviceIdType.MESH
F32 = jnp.float32
BF16 = jnp.bfloat16
NT = (((1,), (1,)), ((), ()))


def iota(shape, dim):
    return lax.broadcasted_iota(jnp.int32, shape, dim)


def first_source(b):
    return min(128 * b // ROWS, PEERS - 12)


def first_rest(b):
    return min(REST * first_source(b) // 16 * 16, PEERS * REST - KREST)


def same_frequency():
    return (iota((SIDE, SIDE), 0) // 2) % GROUP == (iota((SIDE, SIDE), 1) // 2) % GROUP


def spread():
    row, col = iota((SIDE, 2 * BLOCKS), 0), iota((SIDE, 2 * BLOCKS), 1)
    return (col % BLOCKS == row // (2 * GROUP)) & (col // BLOCKS == row % 2)


def first_part(shape):
    return iota(shape, len(shape) - 1) % 2 == 0


def sum_frequencies(m):
    m = m.reshape(BLOCKS, 2 * GROUP, SIDE)
    m = m[:, :8, :] + m[:, 8:, :]
    m = m + pltpu.roll(m, 4, 1)
    return m + pltpu.roll(m, 2, 1)


def first_rows(m, h3):
    m = m.reshape(BLOCKS * 8, SIDE)
    for half in range(2):
        h3[half] = m[:, 128 * half : 128 * half + 128]
    return jnp.concatenate([h3[half, pl.ds(0, BLOCKS, stride=8), :] for half in range(2)], axis=1)


def make_table(fid):
    row = iota((TROWS, FREQS), 0) // 2
    freq = jnp.sum(
        jnp.where(row == iota((TROWS, FREQS), 1), fid.astype(F32), 0.0), axis=1, keepdims=True
    ).astype(jnp.int32)
    t = iota((TROWS, NFFT), 1)
    r = iota((TROWS, NFFT), 0)
    residue = (freq * t + 64 * (r % 2)) % NFFT
    hann = 0.5 - 0.5 * jnp.cos(2.0 * math.pi * t.astype(F32) / NFFT)
    table = hann * jnp.cos(2.0 * math.pi * residue.astype(F32) / NFFT)
    return jnp.where(r // 2 < FREQS, table, 0.0).astype(BF16)


def column_times(b):
    col = iota((1, KMAIN + KREST), 1)
    main = ROWS * (first_source(b) + col // MAIN) + col % MAIN
    rest = col - KMAIN
    rest = ROWS * (first_rest(b) // REST + rest // REST) + MAIN + rest % REST
    return jnp.where(col < KMAIN, main, rest)


def halves(m):
    high = m.astype(BF16)
    return high, (m - high.astype(F32)).astype(BF16)


def product(a, b):
    dot = functools.partial(jnp.dot, preferred_element_type=F32)
    return dot(a[0], b[0]) + (dot(a[0], b[1]) + dot(a[1], b[0]))


def fold(h):
    h = h[:, :128] + pltpu.roll(h[:, 128:], 2, 1)
    return h[:8] + pltpu.roll(h[8:], 4, 1)


def unfold(q):
    h = jnp.concatenate([q, pltpu.roll(q, 124, 1)], axis=0)
    keep = iota((BLOCKS, 128), 1) % 16 < 2
    return jnp.concatenate(
        [jnp.where(keep, h, 0.0), jnp.where(keep, pltpu.roll(h, 126, 1), 0.0)], axis=1
    )


def solve_roots(h, group, h3):
    lane = iota((1, SIDE), 1)
    even = lane % 2 == 0
    diag = (iota((BLOCKS, SIDE), 0) == iota((BLOCKS, SIDE), 1) // (2 * GROUP)) & even
    trace = jnp.sum(jnp.where(diag, h, 0.0), axis=0, keepdims=True)
    trace = jnp.broadcast_to(trace, (8, SIDE))
    for step in (16, 32, 64, 128):
        trace = trace + pltpu.roll(trace, step, 1)
    trace = (trace + pltpu.roll(trace, 1, 1))[:1]
    trace = jnp.where(group * GROUP + (lane // 2) % GROUP < FREQS, trace, 1.0)
    rows = jnp.concatenate(
        [
            jnp.where(even, h, -h),
            jnp.where(even, pltpu.roll(h, SIDE - 1, 1), pltpu.roll(h, 1, 1)),
        ],
        axis=0,
    )
    rows = halves(rows / trace)
    pick = spread().astype(F32).astype(BF16)
    approx = sum(jnp.dot(pick, part, preferred_element_type=F32) for part in rows)
    approx = jnp.where(same_frequency(), approx, 0.0)
    eye = jnp.where(iota((SIDE, SIDE), 0) == iota((SIDE, SIDE), 1), 1.5, 0.0)
    update = eye - 0.5 * approx
    root, approx, update = halves(update), halves(approx), halves(update)
    for step in range(1, ITERS):
        approx = halves(product(approx, update))
        update = halves(eye - 0.5 * product(root, approx))
        root = product(update, root)
        if step < ITERS - 1:
            root = halves(root)
    return (first_rows(sum_frequencies(root), h3) * (1.0 / jnp.sqrt(trace))).astype(BF16)


def spectra_kernel(
    x, w, fid, starts, spec, hc, expand, same, order, root,
    xs, pk, xm, xr, xu, tab, gram, hsend, r1, h2, r2, h8, r18, h28, r28, solved, hcs, h3,
    in_sem, own_main, own_rest, send_main, send_rest, recv_main, recv_rest,
    s1_send, s1_recv, s2_send, s2_recv, s3_send, s3_recv,
):
    y, z, c = (lax.axis_index(a) for a in PTS)
    xx = lax.axis_index("frq")
    me = (y * NZ + z) * NC + c
    load = pltpu.make_async_copy(x, xs, in_sem)
    load.start()

    def at(dx, dy, dz, dc):
        return {
            "pts_0": (y + dy) % NY, "pts_1": (z + dz) % NZ, "pts_2": (c + dc) % NC,
            "frq": (xx + dx) % NX,
        }

    def plane(k):
        j, dy, dc = k % 8, (k // 8) % 4, k // 32
        dz = (1 - j % 2) * (j // 2) + (j % 2) * (8 - (j + 1) // 2)
        return at(0, dy, dz, dc)

    barrier = pltpu.get_barrier_semaphore()

    ys, zs = [lax.rem(y + d, NY) for d in range(NY)], [lax.rem(z + d, NZ) for d in range(NZ)]
    cs, xxs = [c, 1 - c], [lax.rem(xx + d, NX) for d in range(NX)]
    steps = [(0, k // 16, k // 2 % 8, k % 2) for k in range(1, PEERS)]
    steps += [(1 + k // 4, k % 4, 0, 0) for k in range(12)]
    sizes = (NX, NY, NZ, NC)
    for dx, dy, dz, dc in sorted(steps, key=lambda d: -sum(min(i, n - i) for i, n in zip(d, sizes))):
        pl.semaphore_signal(
            barrier, inc=1, device_id_type=MESH,
            device_id={"pts_0": ys[dy], "pts_1": zs[dz], "pts_2": cs[dc], "frq": xxs[dx]},
        )
    load.wait()

    low = iota((8, HALF), 0) < 4

    def pack(q, carry):
        for ch in range(CHUNKS):
            left = xs[MAIN:ROWS, pl.ds(pl.multiple_of(q * POINTS + ch * W, 128), HALF)]
            right = xs[MAIN:ROWS, pl.ds(pl.multiple_of(q * POINTS + ch * W + HALF, 128), HALF)]
            pk[q, ch] = jnp.concatenate([left.astype(F32), right.astype(F32)], axis=0).astype(BF16)
        return carry

    lax.fori_loop(0, PEERS, pack, 0)
    pl.semaphore_wait(barrier, PEERS - 1 + 12)

    for ch in range(CHUNKS):
        pltpu.make_async_copy(
            xs.at[0:MAIN, pl.ds(pl.multiple_of(me * POINTS + ch * W, 128), W)],
            xm.at[ch, pl.ds(pl.multiple_of(me * MAIN, MAIN), MAIN), :],
            own_main.at[ch],
        ).start()
        pltpu.make_async_copy(pk.at[me, ch], xr.at[ch, me], own_rest.at[ch]).start()

        def send(k, carry):
            to = plane(k)
            q = (to["pts_0"] * NZ + to["pts_1"]) * NC + to["pts_2"]
            pltpu.make_async_remote_copy(
                src_ref=xs.at[0:MAIN, pl.ds(pl.multiple_of(q * POINTS + ch * W, 128), W)],
                dst_ref=xm.at[ch, pl.ds(pl.multiple_of(me * MAIN, MAIN), MAIN), :],
                send_sem=send_main.at[ch], recv_sem=recv_main.at[ch],
                device_id=to, device_id_type=MESH,
            ).start()
            pltpu.make_async_remote_copy(
                src_ref=pk.at[q, ch], dst_ref=xr.at[ch, me],
                send_sem=send_rest.at[ch], recv_sem=recv_rest.at[ch],
                device_id=to, device_id_type=MESH,
            ).start()
            return carry

        lax.fori_loop(1, PEERS, send, 0)

    table = make_table(fid[...])
    tau = iota((NFFT, KMAIN + KREST), 0)
    for b in range(BLOCKS):
        pick = jnp.where(tau == column_times(b) - starts[b], 1.0, 0.0).astype(BF16)
        tab[b] = jnp.dot(table, pick, preferred_element_type=F32).astype(BF16)

    def finished(ref, sem):
        pltpu.make_async_copy(ref, ref, sem).wait()

    gram[...] = jnp.zeros_like(gram)
    expand[...] = spread().astype(F32).astype(BF16)
    row, col = iota((SIDE, SIDE), 0), iota((SIDE, SIDE), 1)
    same[...] = jnp.where(row // 32 == (col // 2) % GROUP, 1.0, 0.0)
    order[...] = jnp.where(
        row == (col % 16) * 16 + (col // 32) * 2 + (col // 16) % 2, 1.0, 0.0
    ).astype(BF16)
    root[...] = jnp.sqrt(w[...])

    def chunk(ch, carry):
        here = pl.ds(pl.multiple_of(ch * W, W), W)
        finished(xm.at[ch, pl.ds(0, MAIN), :], own_main.at[ch])
        finished(xr.at[ch, 0], own_rest.at[ch])
        finished(xm.at[ch, pl.ds(0, (PEERS - 1) * MAIN), :], recv_main.at[ch])
        finished(xr.at[ch, pl.ds(0, PEERS - 1)], recv_rest.at[ch])
        rest = xr[ch].astype(F32).reshape(PEERS // 2, 2, 8, HALF)
        first, second = rest[:, 0], rest[:, 1]
        top = iota((PEERS // 2, 8, HALF), 1) < 4
        left = jnp.where(top, first, pltpu.roll(second, 4, 1))
        right = jnp.where(top, pltpu.roll(first, 4, 1), second)
        xu[:, :HALF] = left.reshape(PEERS * REST, HALF).astype(BF16)
        xu[:, HALF:] = right.reshape(PEERS * REST, HALF).astype(BF16)
        for b in range(BLOCKS):
            s0, r0 = MAIN * first_source(b), first_rest(b)
            part = jnp.concatenate([xm[ch, s0 : s0 + KMAIN, :], xu[r0 : r0 + KREST, :]], axis=0)
            rows = jnp.dot(tab[b], part, preferred_element_type=F32).astype(BF16)
            for g in range(GROUPS):
                spec[g, 16 * b : 16 * b + 16, here] = rows[16 * g : 16 * g + 16, :]
        weight = w[:, here]
        for g in range(GROUPS):
            s = spec[g, :, here]
            weighted = (s.astype(F32) * weight).astype(BF16)
            gram[g] += lax.dot_general(s, weighted, NT, preferred_element_type=F32)
        return carry

    lax.fori_loop(0, CHUNKS, chunk, 0)

    mine = jnp.where(c == 0, z, GROUPS - 1)
    large = c == 0
    small = (c == 1) & (z == 0)
    here = z * NC + c
    there = xx * NY + y

    def stage1(g):
        oz, oc = (g, 0) if g < NZ else (0, 1)
        return pltpu.make_async_remote_copy(
            src_ref=hsend.at[g] if g < NZ else h8, dst_ref=(r1 if g < NZ else r18).at[here],
            send_sem=s1_send.at[g], recv_sem=s1_recv,
            device_id={"pts_0": y, "pts_1": oz, "pts_2": oc, "frq": xx}, device_id_type=MESH,
        )

    def elsewhere(g):
        return (z != g) | (c != 0) if g < NZ else (z != 0) | (c != 1)

    def begin1(g):
        @pl.when(elsewhere(g))
        def _():
            stage1(g).start()

    mask = same_frequency()
    even3 = first_part((BLOCKS, 8, SIDE))
    for g in reversed(range(GROUPS)):
        m = sum_frequencies(jnp.where(mask, gram[g], 0.0))
        other = pltpu.roll(m, 7, 1)
        m = jnp.where(even3, m + pltpu.roll(other, SIDE - 1, 2), m - pltpu.roll(other, 1, 2))
        m = first_rows(m, h3.at[g % 2]) * (1.0 / TOTAL)
        if g < NZ:
            hsend[g] = m
            begin1(g + 1)
        else:
            h8[...] = fold(m)
    begin1(0)

    def stage2(k, src, dst):
        return pltpu.make_async_remote_copy(
            src_ref=src, dst_ref=dst.at[there], send_sem=s2_send, recv_sem=s2_recv,
            device_id=at(k // 4, k % 4, 0, 0), device_id_type=MESH,
        )

    def reduced(own, first, total, second):
        first[here] = own
        finished(first.at[pl.ds(0, 15)], s1_recv)
        total[...] = sum((first[i] for i in range(1, 16)), first[0])
        second[there] = total[...]

        def send(k, carry):
            stage2(k, total, second).start()
            return carry

        lax.fori_loop(1, 16, send, 0)
        finished(second.at[pl.ds(0, 15)], s2_recv)
        finished(second.at[pl.ds(0, 15)], s2_send)
        return sum((second[i] for i in range(1, 16)), second[0])

    def stage3(k):
        return pltpu.make_async_remote_copy(
            src_ref=hcs, dst_ref=hc.at[mine], send_sem=s3_send, recv_sem=s3_recv.at[mine],
            device_id=at(0, 0, k // 2, k % 2), device_id_type=MESH,
        )

    @pl.when(large)
    def _():
        solved[...] = reduced(hsend[z], r1, h2, r2)

    @pl.when(small)
    def _():
        solved[...] = unfold(reduced(h8[...], r18, h28, r28))

    @pl.when(large | small)
    def _():
        coefs = solve_roots(solved[...], mine, h3.at[0])
        hcs[...] = coefs
        hc[mine] = coefs

        def out3(k, carry):
            stage3(k).start()
            return carry

        lax.fori_loop(1, 16, out3, 0)

    for g in range(GROUPS):
        @pl.when(elsewhere(g))
        def _():
            stage1(g).wait_send()
            finished(hc.at[g], s3_recv.at[g])

    @pl.when(large | small)
    def _():
        finished(xm.at[0, pl.ds(0, 15 * BLOCKS), :], s3_send)

    for ch in range(CHUNKS):
        finished(xm.at[ch, pl.ds(0, (PEERS - 1) * MAIN), :], send_main.at[ch])
        finished(xr.at[ch, pl.ds(0, PEERS - 1)], send_rest.at[ch])


def project_kernel(hc, s, expand, same, order, root, out, fields, matrices, sem):
    coefs = hc[...].astype(F32).reshape(GROUPS * BLOCKS, SIDE).astype(BF16)
    coefs = jnp.dot(coefs, order[...], preferred_element_type=F32)
    real = (iota((1, SIDE), 1) // BLOCKS) % 2 == 0
    for g in range(GROUPS):
        h = coefs[BLOCKS * g : BLOCKS * (g + 1)]
        rows = jnp.concatenate(
            [
                jnp.where(real, h, -h),
                jnp.where(real, pltpu.roll(h, SIDE - BLOCKS, 1), pltpu.roll(h, BLOCKS, 1)),
            ],
            axis=0,
        ).astype(BF16)
        matrix = lax.dot_general(
            rows, expand[...], (((0,), (1,)), ((), ())), preferred_element_type=F32
        )
        matrices[g] = (matrix * same[...]).astype(BF16)
    copies = []
    for g in range(GROUPS):
        count = min(SIDE, (FREQS - g * GROUP) * 2 * BLOCKS)
        field = jnp.dot(matrices[g, :count, :], s[g], preferred_element_type=F32)
        fields[g, :count] = (field * root[...]).astype(BF16)
        copies.append(
            pltpu.make_async_copy(
                fields.at[g, pl.ds(0, count)], out.at[pl.ds(g * SIDE, count)], sem.at[g]
            )
        )
        copies[-1].start()
    for copy in copies:
        copy.wait()


def shards(snapshots, weights, freq_ids, starts):
    vmem = pl.BlockSpec(memory_space=pltpu.VMEM)
    anywhere = pl.BlockSpec(memory_space=pl.ANY)
    dma = pltpu.SemaphoreType.DMA
    spectra, coefs, *shared = pl.pallas_call(
        spectra_kernel,
        name="exchange_spectra",
        out_shape=(
            pltpu.VMEM((GROUPS, SIDE, POINTS), BF16),
            pltpu.VMEM((GROUPS, BLOCKS, SIDE), BF16),
            pltpu.VMEM((SIDE, 2 * BLOCKS), BF16),
            pltpu.VMEM((SIDE, SIDE), F32),
            pltpu.VMEM((SIDE, SIDE), BF16),
            pltpu.VMEM((1, POINTS), F32),
        ),
        in_specs=[anywhere, vmem, vmem, pl.BlockSpec(memory_space=pltpu.SMEM)],
        out_specs=(vmem,) * 6,
        scratch_shapes=[
            pltpu.VMEM((ROWS, PEERS * POINTS), BF16),
            pltpu.VMEM((PEERS, CHUNKS, 8, HALF), BF16),
            pltpu.VMEM((CHUNKS, PEERS * MAIN, W), BF16),
            pltpu.VMEM((CHUNKS, PEERS, 8, HALF), BF16),
            pltpu.VMEM((PEERS * REST, W), BF16),
            pltpu.VMEM((BLOCKS, TROWS, KMAIN + KREST), BF16),
            pltpu.VMEM((GROUPS, SIDE, SIDE), F32),
            pltpu.VMEM((NZ, BLOCKS, SIDE), F32),
            pltpu.VMEM((16, BLOCKS, SIDE), F32),
            pltpu.VMEM((BLOCKS, SIDE), F32),
            pltpu.VMEM((16, BLOCKS, SIDE), F32),
            pltpu.VMEM((8, 128), F32),
            pltpu.VMEM((16, 8, 128), F32),
            pltpu.VMEM((8, 128), F32),
            pltpu.VMEM((16, 8, 128), F32),
            pltpu.VMEM((BLOCKS, SIDE), F32),
            pltpu.VMEM((BLOCKS, SIDE), BF16),
            pltpu.VMEM((2, 2, BLOCKS * 8, 128), F32),
            dma(()), dma((CHUNKS,)), dma((CHUNKS,)), dma((CHUNKS,)), dma((CHUNKS,)),
            dma((CHUNKS,)), dma((CHUNKS,)),
            dma((GROUPS,)), dma(()), dma(()), dma(()), dma(()), dma((GROUPS,)),
        ],
        compiler_params=pltpu.CompilerParams(
            collective_id=0, has_side_effects=True, vmem_limit_bytes=56 << 20
        ),
    )(snapshots.reshape(ROWS, PEERS * POINTS), weights, freq_ids.reshape(1, FREQS), starts)
    field = pl.pallas_call(
        project_kernel,
        name="project_modes",
        out_shape=jax.ShapeDtypeStruct((FREQS * 2 * BLOCKS, POINTS), BF16),
        in_specs=[vmem] * 6,
        out_specs=anywhere,
        scratch_shapes=[
            pltpu.VMEM((GROUPS, SIDE, POINTS), BF16),
            pltpu.VMEM((GROUPS, SIDE, SIDE), BF16),
            dma((GROUPS,)),
        ],
        compiler_params=pltpu.CompilerParams(vmem_limit_bytes=24 << 20),
    )(coefs, spectra, *shared)
    return field.reshape(FREQS, 2, BLOCKS, 1, POINTS)


def solution(mesh):
    torus = Mesh(
        mesh.devices.reshape(NY, NZ, NC, mesh.shape["frq"]), ("pts_0", "pts_1", "pts_2", "frq")
    )
    placed = (P(PTS, "frq", None), P("frq", PTS), P(), P())
    return jax.shard_map(
        shards,
        mesh=torus,
        in_specs=placed,
        out_specs=P(None, None, None, "frq", PTS),
        check_vma=False,
    )
```

```python
import functools
import math

import jax
import jax.numpy as jnp
from jax import lax
from jax.experimental import pallas as pl
from jax.experimental.pallas import tpu as pltpu
from jax.sharding import Mesh
from jax.sharding import PartitionSpec as P

NFFT = 256
ITERS = 3
PTS = ("pts_0", "pts_1", "pts_2")
NY, NZ, NC, NX = 4, 8, 2, 4
PEERS = NY * NZ * NC
ROWS = 36
MAIN = 32
REST = ROWS - MAIN
BLOCKS = 16
FREQS = 65
GROUP = 8
GROUPS = 9
SIDE = BLOCKS * GROUP * 2
TROWS = GROUPS * GROUP * 2
POINTS = 1024
CHUNKS = 4
W = POINTS // CHUNKS
HALF = W // 2
KMAIN = 12 * MAIN
KREST = 64
TOTAL = 262144
MESH = pl.DeviceIdType.MESH
F32 = jnp.float32
BF16 = jnp.bfloat16
NT = (((1,), (1,)), ((), ()))


def iota(shape, dim):
    return lax.broadcasted_iota(jnp.int32, shape, dim)


def first_source(b):
    return min(128 * b // ROWS, PEERS - 12)


def first_rest(b):
    return min(REST * first_source(b) // 16 * 16, PEERS * REST - KREST)


def same_frequency():
    return (iota((SIDE, SIDE), 0) // 2) % GROUP == (iota((SIDE, SIDE), 1) // 2) % GROUP


def spread():
    row, col = iota((SIDE, 2 * BLOCKS), 0), iota((SIDE, 2 * BLOCKS), 1)
    return (col % BLOCKS == row // (2 * GROUP)) & (col // BLOCKS == row % 2)


def first_part(shape):
    return iota(shape, len(shape) - 1) % 2 == 0


def sum_frequencies(m):
    m = m.reshape(BLOCKS, 2 * GROUP, SIDE)
    m = m[:, :8, :] + m[:, 8:, :]
    m = m + pltpu.roll(m, 4, 1)
    return m + pltpu.roll(m, 2, 1)


def first_rows(m, h3):
    m = m.reshape(BLOCKS * 8, SIDE)
    for half in range(2):
        h3[half] = m[:, 128 * half : 128 * half + 128]
    return jnp.concatenate([h3[half, pl.ds(0, BLOCKS, stride=8), :] for half in range(2)], axis=1)


def make_table(fid):
    row = iota((TROWS, FREQS), 0) // 2
    freq = jnp.sum(
        jnp.where(row == iota((TROWS, FREQS), 1), fid.astype(F32), 0.0), axis=1, keepdims=True
    ).astype(jnp.int32)
    t = iota((TROWS, NFFT), 1)
    r = iota((TROWS, NFFT), 0)
    residue = (freq * t + 64 * (r % 2)) % NFFT
    hann = 0.5 - 0.5 * jnp.cos(2.0 * math.pi * t.astype(F32) / NFFT)
    table = hann * jnp.cos(2.0 * math.pi * residue.astype(F32) / NFFT)
    return jnp.where(r // 2 < FREQS, table, 0.0).astype(BF16)


def column_times(b):
    col = iota((1, KMAIN + KREST), 1)
    main = ROWS * (first_source(b) + col // MAIN) + col % MAIN
    rest = col - KMAIN
    rest = ROWS * (first_rest(b) // REST + rest // REST) + MAIN + rest % REST
    return jnp.where(col < KMAIN, main, rest)


def far_first(sizes):
    def distance(k):
        return sum(min(i, n - i) for i, n in zip((k // sizes[1], k % sizes[1]), sizes))

    return sorted(range(1, sizes[0] * sizes[1]), key=lambda k: -distance(k))


def halves(m):
    high = m.astype(BF16)
    return high, (m - high.astype(F32)).astype(BF16)


def product(a, b):
    dot = functools.partial(jnp.dot, preferred_element_type=F32)
    return dot(a[0], b[0]) + (dot(a[0], b[1]) + dot(a[1], b[0]))


def fold(h):
    h = h[:, :128] + pltpu.roll(h[:, 128:], 2, 1)
    return h[:8] + pltpu.roll(h[8:], 4, 1)


def unfold(q):
    h = jnp.concatenate([q, pltpu.roll(q, 124, 1)], axis=0)
    keep = iota((BLOCKS, 128), 1) % 16 < 2
    return jnp.concatenate(
        [jnp.where(keep, h, 0.0), jnp.where(keep, pltpu.roll(h, 126, 1), 0.0)], axis=1
    )


def solve_roots(h, group, h3):
    lane = iota((1, SIDE), 1)
    even = lane % 2 == 0
    diag = (iota((BLOCKS, SIDE), 0) == iota((BLOCKS, SIDE), 1) // (2 * GROUP)) & even
    trace = jnp.sum(jnp.where(diag, h, 0.0), axis=0, keepdims=True)
    trace = jnp.broadcast_to(trace, (8, SIDE))
    for step in (16, 32, 64, 128):
        trace = trace + pltpu.roll(trace, step, 1)
    trace = (trace + pltpu.roll(trace, 1, 1))[:1]
    trace = jnp.where(group * GROUP + (lane // 2) % GROUP < FREQS, trace, 1.0)
    rows = jnp.concatenate(
        [
            jnp.where(even, h, -h),
            jnp.where(even, pltpu.roll(h, SIDE - 1, 1), pltpu.roll(h, 1, 1)),
        ],
        axis=0,
    )
    rows = halves(rows / trace)
    pick = spread().astype(F32).astype(BF16)
    approx = sum(jnp.dot(pick, part, preferred_element_type=F32) for part in rows)
    approx = jnp.where(same_frequency(), approx, 0.0)
    eye = jnp.where(iota((SIDE, SIDE), 0) == iota((SIDE, SIDE), 1), 1.5, 0.0)
    update = eye - 0.5 * approx
    root, approx, update = halves(update), halves(approx), halves(update)
    for step in range(1, ITERS):
        approx = halves(product(approx, update))
        update = halves(eye - 0.5 * product(root, approx))
        root = product(update, root)
        if step < ITERS - 1:
            root = halves(root)
    return (first_rows(sum_frequencies(root), h3) * (1.0 / jnp.sqrt(trace))).astype(BF16)


def spectra_kernel(
    x, w_in, fid_in, starts, spec, hc, expand, same, order, root,
    xs, pk, xm, xr, xu, tab, gram, hsend, r1, h2, r2, h8, r18, h28, r28, solved, hcs, h3, w, fid,
    in_sem, small_sem, own_main, own_rest, send_main, send_rest, recv_main, recv_rest,
    s1_send, s1_recv, s2_send, s2_recv, s3_send, s3_recv,
):
    y, z, c = (lax.axis_index(a) for a in PTS)
    xx = lax.axis_index("frq")
    me = (y * NZ + z) * NC + c
    load = pltpu.make_async_copy(x, xs, in_sem)
    load.start()
    small_loads = [
        pltpu.make_async_copy(w_in, w, small_sem.at[0]),
        pltpu.make_async_copy(fid_in, fid, small_sem.at[1]),
    ]
    for copy in small_loads:
        copy.start()

    def at(dx, dy, dz, dc):
        return {
            "pts_0": (y + dy) % NY, "pts_1": (z + dz) % NZ, "pts_2": (c + dc) % NC,
            "frq": (xx + dx) % NX,
        }

    def plane(k):
        j, dy, dc = k % 8, (k // 8) % 4, k // 32
        dz = (1 - j % 2) * (j // 2) + (j % 2) * (8 - (j + 1) // 2)
        return at(0, dy, dz, dc)

    barrier = pltpu.get_barrier_semaphore()

    ys, zs = [lax.rem(y + d, NY) for d in range(NY)], [lax.rem(z + d, NZ) for d in range(NZ)]
    cs, xxs = [c, 1 - c], [lax.rem(xx + d, NX) for d in range(NX)]
    steps = [(0, k // 16, k // 2 % 8, k % 2) for k in range(1, PEERS)]
    steps += [(1 + k // 4, k % 4, 0, 0) for k in range(12)]
    sizes = (NX, NY, NZ, NC)
    for dx, dy, dz, dc in sorted(steps, key=lambda d: -sum(min(i, n - i) for i, n in zip(d, sizes))):
        pl.semaphore_signal(
            barrier, inc=1, device_id_type=MESH,
            device_id={"pts_0": ys[dy], "pts_1": zs[dz], "pts_2": cs[dc], "frq": xxs[dx]},
        )
    load.wait()

    low = iota((8, HALF), 0) < 4

    def pack(q, carry):
        for ch in range(CHUNKS):
            left = xs[MAIN:ROWS, pl.ds(pl.multiple_of(q * POINTS + ch * W, 128), HALF)]
            right = xs[MAIN:ROWS, pl.ds(pl.multiple_of(q * POINTS + ch * W + HALF, 128), HALF)]
            pk[q, ch] = jnp.concatenate([left.astype(F32), right.astype(F32)], axis=0).astype(BF16)
        return carry

    lax.fori_loop(0, PEERS, pack, 0)
    pl.semaphore_wait(barrier, PEERS - 1 + 12)

    for ch in range(CHUNKS):
        pltpu.make_async_copy(
            xs.at[0:MAIN, pl.ds(pl.multiple_of(me * POINTS + ch * W, 128), W)],
            xm.at[ch, pl.ds(pl.multiple_of(me * MAIN, MAIN), MAIN), :],
            own_main.at[ch],
        ).start()
        pltpu.make_async_copy(pk.at[me, ch], xr.at[ch, me], own_rest.at[ch]).start()

        def send(k, carry):
            to = plane(k)
            q = (to["pts_0"] * NZ + to["pts_1"]) * NC + to["pts_2"]
            pltpu.make_async_remote_copy(
                src_ref=xs.at[0:MAIN, pl.ds(pl.multiple_of(q * POINTS + ch * W, 128), W)],
                dst_ref=xm.at[ch, pl.ds(pl.multiple_of(me * MAIN, MAIN), MAIN), :],
                send_sem=send_main.at[ch], recv_sem=recv_main.at[ch],
                device_id=to, device_id_type=MESH,
            ).start()
            pltpu.make_async_remote_copy(
                src_ref=pk.at[q, ch], dst_ref=xr.at[ch, me],
                send_sem=send_rest.at[ch], recv_sem=recv_rest.at[ch],
                device_id=to, device_id_type=MESH,
            ).start()
            return carry

        lax.fori_loop(1, PEERS, send, 0)

    for copy in small_loads:
        copy.wait()
    table = make_table(fid[...])
    tau = iota((NFFT, KMAIN + KREST), 0)
    for b in range(BLOCKS):
        pick = jnp.where(tau == column_times(b) - starts[b], 1.0, 0.0).astype(BF16)
        tab[b] = jnp.dot(table, pick, preferred_element_type=F32).astype(BF16)

    def finished(ref, sem):
        pltpu.make_async_copy(ref, ref, sem).wait()

    gram[...] = jnp.zeros_like(gram)
    expand[...] = spread().astype(F32).astype(BF16)
    row, col = iota((SIDE, SIDE), 0), iota((SIDE, SIDE), 1)
    same[...] = jnp.where(row // 32 == (col // 2) % GROUP, 1.0, 0.0)
    order[...] = jnp.where(
        row == (col % 16) * 16 + (col // 32) * 2 + (col // 16) % 2, 1.0, 0.0
    ).astype(BF16)
    root[...] = jnp.sqrt(w[...])

    def chunk(ch, carry):
        here = pl.ds(pl.multiple_of(ch * W, W), W)
        finished(xm.at[ch, pl.ds(0, MAIN), :], own_main.at[ch])
        finished(xr.at[ch, 0], own_rest.at[ch])
        finished(xm.at[ch, pl.ds(0, (PEERS - 1) * MAIN), :], recv_main.at[ch])
        finished(xr.at[ch, pl.ds(0, PEERS - 1)], recv_rest.at[ch])
        rest = xr[ch].astype(F32).reshape(PEERS // 2, 2, 8, HALF)
        first, second = rest[:, 0], rest[:, 1]
        top = iota((PEERS // 2, 8, HALF), 1) < 4
        left = jnp.where(top, first, pltpu.roll(second, 4, 1))
        right = jnp.where(top, pltpu.roll(first, 4, 1), second)
        xu[:, :HALF] = left.reshape(PEERS * REST, HALF).astype(BF16)
        xu[:, HALF:] = right.reshape(PEERS * REST, HALF).astype(BF16)
        for b in range(BLOCKS):
            s0, r0 = MAIN * first_source(b), first_rest(b)
            part = jnp.concatenate([xm[ch, s0 : s0 + KMAIN, :], xu[r0 : r0 + KREST, :]], axis=0)
            rows = jnp.dot(tab[b], part, preferred_element_type=F32).astype(BF16)
            for g in range(GROUPS):
                spec[g, 16 * b : 16 * b + 16, here] = rows[16 * g : 16 * g + 16, :]
        weight = w[:, here]
        for g in range(GROUPS):
            s = spec[g, :, here]
            weighted = (s.astype(F32) * weight).astype(BF16)
            gram[g] += lax.dot_general(s, weighted, NT, preferred_element_type=F32)
        return carry

    lax.fori_loop(0, CHUNKS, chunk, 0)

    mine = jnp.where(c == 0, z, GROUPS - 1)
    large = c == 0
    small = (c == 1) & (z == 0)
    here = z * NC + c
    there = xx * NY + y

    def stage1(g):
        oz, oc = (g, 0) if g < NZ else (0, 1)
        return pltpu.make_async_remote_copy(
            src_ref=hsend.at[g] if g < NZ else h8, dst_ref=(r1 if g < NZ else r18).at[here],
            send_sem=s1_send.at[g], recv_sem=s1_recv,
            device_id={"pts_0": y, "pts_1": oz, "pts_2": oc, "frq": xx}, device_id_type=MESH,
        )

    def elsewhere(g):
        return (z != g) | (c != 0) if g < NZ else (z != 0) | (c != 1)

    def begin1(g):
        @pl.when(elsewhere(g))
        def _():
            stage1(g).start()

    mask = same_frequency()
    even3 = first_part((BLOCKS, 8, SIDE))
    for g in reversed(range(GROUPS)):
        m = sum_frequencies(jnp.where(mask, gram[g], 0.0))
        other = pltpu.roll(m, 7, 1)
        m = jnp.where(even3, m + pltpu.roll(other, SIDE - 1, 2), m - pltpu.roll(other, 1, 2))
        m = first_rows(m, h3.at[g % 2]) * (1.0 / TOTAL)
        if g < NZ:
            hsend[g] = m
            begin1(g + 1)
        else:
            h8[...] = fold(m)
    begin1(0)

    def stage2(k, src, dst):
        return pltpu.make_async_remote_copy(
            src_ref=src, dst_ref=dst.at[there], send_sem=s2_send, recv_sem=s2_recv,
            device_id={
                "pts_0": ys[k % 4], "pts_1": z, "pts_2": c, "frq": xxs[k // 4],
            },
            device_id_type=MESH,
        )

    def reduced(own, first, total, second):
        first[here] = own
        finished(first.at[pl.ds(0, 15)], s1_recv)
        total[...] = sum((first[i] for i in range(1, 16)), first[0])
        second[there] = total[...]

        for k in far_first((NX, NY)):
            stage2(k, total, second).start()
        finished(second.at[pl.ds(0, 15)], s2_recv)
        result = sum((second[i] for i in range(1, 16)), second[0])
        finished(second.at[pl.ds(0, 15)], s2_send)
        return result

    def stage3(k):
        return pltpu.make_async_remote_copy(
            src_ref=hcs, dst_ref=hc.at[mine], send_sem=s3_send, recv_sem=s3_recv.at[mine],
            device_id={"pts_0": y, "pts_1": zs[k // 2], "pts_2": cs[k % 2], "frq": xx},
            device_id_type=MESH,
        )

    @pl.when(large)
    def _():
        solved[...] = reduced(hsend[z], r1, h2, r2)

    @pl.when(small)
    def _():
        solved[...] = unfold(reduced(h8[...], r18, h28, r28))

    @pl.when(large | small)
    def _():
        coefs = solve_roots(solved[...], mine, h3.at[0])
        hcs[...] = coefs
        hc[mine] = coefs

        for k in far_first((NZ, NC)):
            stage3(k).start()

    for g in range(GROUPS):
        @pl.when(elsewhere(g))
        def _():
            stage1(g).wait_send()
            finished(hc.at[g], s3_recv.at[g])

    @pl.when(large | small)
    def _():
        finished(xm.at[0, pl.ds(0, 15 * BLOCKS), :], s3_send)

    for ch in range(CHUNKS):
        finished(xm.at[ch, pl.ds(0, (PEERS - 1) * MAIN), :], send_main.at[ch])
        finished(xr.at[ch, pl.ds(0, PEERS - 1)], send_rest.at[ch])


def project_kernel(hc, s, expand, same, order, root, out, fields, matrices, sem):
    coefs = hc[...].astype(F32).reshape(GROUPS * BLOCKS, SIDE).astype(BF16)
    coefs = jnp.dot(coefs, order[...], preferred_element_type=F32)
    real = (iota((1, SIDE), 1) // BLOCKS) % 2 == 0
    for g in range(GROUPS):
        h = coefs[BLOCKS * g : BLOCKS * (g + 1)]
        rows = jnp.concatenate(
            [
                jnp.where(real, h, -h),
                jnp.where(real, pltpu.roll(h, SIDE - BLOCKS, 1), pltpu.roll(h, BLOCKS, 1)),
            ],
            axis=0,
        ).astype(BF16)
        matrix = lax.dot_general(
            rows, expand[...], (((0,), (1,)), ((), ())), preferred_element_type=F32
        )
        matrices[g] = (matrix * same[...]).astype(BF16)
    copies = []
    for g in range(GROUPS):
        count = min(SIDE, (FREQS - g * GROUP) * 2 * BLOCKS)
        field = jnp.dot(matrices[g, :count, :], s[g], preferred_element_type=F32)
        fields[g, :count] = (field * root[...]).astype(BF16)
        copies.append(
            pltpu.make_async_copy(
                fields.at[g, pl.ds(0, count)], out.at[pl.ds(g * SIDE, count)], sem.at[g]
            )
        )
        copies[-1].start()
    for copy in copies:
        copy.wait()


def shards(snapshots, weights, freq_ids, starts):
    vmem = pl.BlockSpec(memory_space=pltpu.VMEM)
    anywhere = pl.BlockSpec(memory_space=pl.ANY)
    dma = pltpu.SemaphoreType.DMA
    spectra, coefs, *shared = pl.pallas_call(
        spectra_kernel,
        name="exchange_spectra",
        out_shape=(
            pltpu.VMEM((GROUPS, SIDE, POINTS), BF16),
            pltpu.VMEM((GROUPS, BLOCKS, SIDE), BF16),
            pltpu.VMEM((SIDE, 2 * BLOCKS), BF16),
            pltpu.VMEM((SIDE, SIDE), F32),
            pltpu.VMEM((SIDE, SIDE), BF16),
            pltpu.VMEM((1, POINTS), F32),
        ),
        in_specs=[anywhere, anywhere, anywhere, pl.BlockSpec(memory_space=pltpu.SMEM)],
        out_specs=(vmem,) * 6,
        scratch_shapes=[
            pltpu.VMEM((ROWS, PEERS * POINTS), BF16),
            pltpu.VMEM((PEERS, CHUNKS, 8, HALF), BF16),
            pltpu.VMEM((CHUNKS, PEERS * MAIN, W), BF16),
            pltpu.VMEM((CHUNKS, PEERS, 8, HALF), BF16),
            pltpu.VMEM((PEERS * REST, W), BF16),
            pltpu.VMEM((BLOCKS, TROWS, KMAIN + KREST), BF16),
            pltpu.VMEM((GROUPS, SIDE, SIDE), F32),
            pltpu.VMEM((NZ, BLOCKS, SIDE), F32),
            pltpu.VMEM((16, BLOCKS, SIDE), F32),
            pltpu.VMEM((BLOCKS, SIDE), F32),
            pltpu.VMEM((16, BLOCKS, SIDE), F32),
            pltpu.VMEM((8, 128), F32),
            pltpu.VMEM((16, 8, 128), F32),
            pltpu.VMEM((8, 128), F32),
            pltpu.VMEM((16, 8, 128), F32),
            pltpu.VMEM((BLOCKS, SIDE), F32),
            pltpu.VMEM((BLOCKS, SIDE), BF16),
            pltpu.VMEM((2, 2, BLOCKS * 8, 128), F32),
            pltpu.VMEM((1, POINTS), F32),
            pltpu.VMEM((1, FREQS), jnp.int32),
            dma(()), dma((2,)), dma((CHUNKS,)), dma((CHUNKS,)), dma((CHUNKS,)), dma((CHUNKS,)),
            dma((CHUNKS,)), dma((CHUNKS,)),
            dma((GROUPS,)), dma(()), dma(()), dma(()), dma(()), dma((GROUPS,)),
        ],
        compiler_params=pltpu.CompilerParams(
            collective_id=0, has_side_effects=True, vmem_limit_bytes=56 << 20
        ),
    )(snapshots.reshape(ROWS, PEERS * POINTS), weights, freq_ids.reshape(1, FREQS), starts)
    field = pl.pallas_call(
        project_kernel,
        name="project_modes",
        out_shape=jax.ShapeDtypeStruct((FREQS * 2 * BLOCKS, POINTS), BF16),
        in_specs=[vmem] * 6,
        out_specs=anywhere,
        scratch_shapes=[
            pltpu.VMEM((GROUPS, SIDE, POINTS), BF16),
            pltpu.VMEM((GROUPS, SIDE, SIDE), BF16),
            dma((GROUPS,)),
        ],
        compiler_params=pltpu.CompilerParams(vmem_limit_bytes=24 << 20),
    )(coefs, spectra, *shared)
    return field.reshape(FREQS, 2, BLOCKS, 1, POINTS)


def solution(mesh):
    torus = Mesh(
        mesh.devices.reshape(NY, NZ, NC, mesh.shape["frq"]), ("pts_0", "pts_1", "pts_2", "frq")
    )
    placed = (P(PTS, "frq", None), P("frq", PTS), P(), P())
    return jax.shard_map(
        shards,
        mesh=torus,
        in_specs=placed,
        out_specs=P(None, None, None, "frq", PTS),
        check_vma=False,
    )
```
